32 devices in a mesh: row: 8 (over z, core), col: 4 (over y, x).
Axes of the slice: x: 2, y: 2, z: 4, core: 2. Of those that a mesh axis runs over, the one named last changes fastest.
Arguments:
- trials: float32 [2, 512, 1024], P(None, 'col', 'row'), may hold values from -6 to 6
- valence_orb: float32 [512, 8192], P('col', 'row'), may hold values from -0.25 to 0.25
- conduction_orb: float32 [1024, 8192], P('row', 'col'), may hold values from -0.1875 to 0.1875
- screened: float32 [8192, 8192], P('row', 'col'), may hold values from -0.5 to 0.5
Outputs:
- applied: float32 [2, 512, 1024], P(None, 'col', 'row')
The draws below stay inside these ranges and needn't reach their ends.
All inputs are finite; a program needn't handle non-finite values.
Results may differ from the reference program's by a relative error of at most 0.0003.
Values sent between devices are 32-bit elements; how exact they have to be, the bound alone decides.
A program may use at most 64 MiB of HBM per device.

```python
import jax
import jax.numpy as jnp
from jax import lax

NT = 2
V = 512
C = 1024
POINTS = 8192


def block_levels(own_key, shape, split, least, high):
    def one(position, parts):
        draws = jax.random.uniform(jax.random.fold_in(jax.random.fold_in(own_key, 6), position), (parts,), jnp.float32, least / len(split), high / len(split))
        return jnp.repeat(jnp.exp(draws), shape[position] // parts).reshape((-1,) + (1,) * (len(shape) - position - 1))

    factor_of = one(*split[0])
    for cut in split[1:]:
        factor_of = factor_of * one(*cut)
    return factor_of


def gaussian(own_key, shape, width, reach, cuts=(), held_as=jnp.bfloat16):
    values = jax.random.normal(own_key, shape, jnp.float32) * width
    if len(cuts) > 0:
        values = block_levels(own_key, shape, cuts, -0.22, 0.18) * values
    return jnp.clip(values, min=-reach, max=reach).astype(held_as)


def setup_inputs(seed: int = 0) -> dict:
    arg_keys = jax.random.split(jax.random.key(seed), 5)
    trials = gaussian(arg_keys[0], (NT, V, C), 1.0, 6.0, ((1, 4), (2, 8)), jnp.float32)
    valence_orb = gaussian(arg_keys[1], (V, POINTS), V ** -0.5, 0.25, ((0, 4), (1, 8)), jnp.float32)
    conduction_orb = gaussian(arg_keys[2], (C, POINTS), C ** -0.5, 0.1875, ((0, 8), (1, 4)), jnp.float32)
    screened = gaussian(arg_keys[3], (POINTS, POINTS), (POINTS * POINTS // (V * C)) ** -0.5, 0.5, ((0, 8), (1, 4)), jnp.float32)
    return dict(trials=trials, valence_orb=valence_orb, conduction_orb=conduction_orb, screened=screened)


def reference(trials, valence_orb, conduction_orb, screened):
    highest = lax.Precision.HIGHEST
    block_rows = min(POINTS, 1024)
    block_count = POINTS // block_rows

    def apply_trial(trial_matrix):
        half_encoded = jnp.dot(trial_matrix, conduction_orb, precision=highest, preferred_element_type=jnp.float32)

        def accumulate(total, index):
            offset = (index * block_rows).astype(jnp.int32)
            valence_block = lax.dynamic_slice_in_dim(valence_orb, offset, block_rows, 1)
            screened_block = lax.dynamic_slice_in_dim(screened, offset, block_rows, 0)
            encoded = jnp.dot(valence_block.T, half_encoded, precision=highest, preferred_element_type=jnp.float32)
            pairs = screened_block * encoded
            return total + jnp.dot(valence_block, pairs, precision=highest, preferred_element_type=jnp.float32), None

        total, unused = lax.scan(accumulate, jnp.zeros((V, POINTS), jnp.float32), jnp.arange(block_count, dtype=jnp.int32))
        return jnp.dot(total, conduction_orb.T, precision=highest, preferred_element_type=jnp.float32)

    return lax.map(apply_trial, trials)
```

```python
import functools

import jax
import jax.numpy as jnp
from jax import lax
from jax.experimental import pallas as pl
from jax.experimental.pallas import tpu as pltpu
from jax.sharding import PartitionSpec as P

F32 = jnp.float32
BF16 = jnp.bfloat16


def split(x):
    hi = x.astype(BF16)
    return hi, (x - hi.astype(F32)).astype(BF16)


def dot3(a_hi, a_lo, b_hi, b_lo, dims=((1,), (0,))):
    def one(a, b):
        return lax.dot_general(a, b, (dims, ((), ())), preferred_element_type=F32)

    return one(a_hi, b_hi) + (one(a_lo, b_hi) + one(a_hi, b_lo))


def kernel(
    R, Q, K,
    t_ref, v_ref, co_ref, s_hbm, out_ref,
    t_buf, t_hi, t_lo, v_all, v_hi, v_lo, vt_hi, vt_lo, co_buf, co_hi, co_lo, s_buf,
    p_hi, p_lo, u_hi, u_lo, psend, precv, osum, xrecv, zbuf, zrecv,
    t_recv, t_zs, t_xs, t_ps, v_recv, v_send, co_recv, co_own, co_rel, co_fwd,
    s_sem, p_send, p_recv, x_send, x_recv, z_send, z_recv,
):
    NT, vb, cb = t_ref.shape
    V = vb * Q
    L = R // 2
    nw = co_buf.shape[3]
    row, q = lax.axis_index("row"), lax.axis_index("col")
    p, c = row // 2, row % 2
    mypos = c * L + p
    partner = (p * 2 + (1 - c), q)

    def line(pp):
        return (pp * 2 + c, q)

    def peer(qq):
        return (row, qq)

    def remote(src, dst, ss, rs, dev):
        return pltpu.make_async_remote_copy(
            src_ref=src, dst_ref=dst, send_sem=ss, recv_sem=rs,
            device_id=dev, device_id_type=pl.DeviceIdType.MESH,
        )

    barrier = pltpu.get_barrier_semaphore()
    others = [partner]
    others += [line((p + d) % L) for d in range(1, L)]
    others += [peer((q + d) % Q) for d in range(1, Q)]
    for dev in others:
        pl.semaphore_signal(barrier, inc=1, device_id=dev, device_id_type=pl.DeviceIdType.MESH)
    pl.semaphore_wait(barrier, len(others))

    def t_line(d):
        return remote(t_ref, t_buf.at[mypos, q], t_zs.at[d], t_recv.at[mypos, q], line((p + d) % L))

    def t_peer(j, d):
        pos = c * L + (p + L - j) % L
        src = t_ref if j == 0 else t_buf.at[pos, q]
        return remote(src, t_buf.at[pos, q], t_xs.at[j, d], t_recv.at[pos, q], peer((q + d) % Q))

    def t_partner(j, d):
        pos = c * L + (p + L - j) % L
        qq = (q + Q - d) % Q
        src = t_ref if (j == 0 and d == 0) else t_buf.at[pos, qq]
        return remote(src, t_buf.at[pos, qq], t_ps.at[j, d], t_recv.at[pos, qq], partner)

    def t_wait(pos, qq):
        remote(t_buf.at[pos, qq], t_buf.at[pos, qq], t_zs.at[0], t_recv.at[pos, qq], partner).wait_recv()

    def v_peer(d):
        return remote(v_ref, v_all.at[q], v_send.at[d], v_recv.at[q], peer((q + d) % Q))

    def own_to(k, d):
        lanes = pl.ds(pl.multiple_of(k * nw, nw), nw)
        sign = 1 if d > 0 else -1
        return remote(
            co_ref.at[:, lanes], co_buf.at[k, mypos],
            co_own.at[k, abs(d) - 1 + (2 if sign < 0 else 0)], co_recv.at[k, mypos],
            line(jnp.clip(p + d, 0, L - 1)),
        )

    def own_partner(k):
        lanes = pl.ds(pl.multiple_of(k * nw, nw), nw)
        return remote(
            co_ref.at[:, lanes], co_buf.at[k, mypos], co_own.at[k, 4], co_recv.at[k, mypos], partner
        )

    def own_cases():
        for d in (1, 2):
            if d < L:
                yield d, p + d <= L - 1
                yield -d, p - d >= 0

    def send_own(k):
        for d, ok in own_cases():
            @pl.when(ok)
            def _():
                own_to(k, d).start()
        own_partner(k).start()

    def relay_right(pp):
        return jnp.logical_and(p - pp >= 2, p < L - 1)

    def relay_left(pp):
        return jnp.logical_and(pp - p >= 2, p > 0)

    def relay_copy(k, pp, to):
        pos = c * L + pp
        return remote(
            co_buf.at[k, pos], co_buf.at[k, pos], co_rel.at[k, pp], co_recv.at[k, pos],
            line(jnp.clip(to, 0, L - 1)),
        )

    def co_wait(k, pos):
        remote(co_buf.at[k, pos], co_buf.at[k, pos], co_own.at[k, 4], co_recv.at[k, pos], partner).wait_recv()

    def relay(k):
        for pp in range(L):
            for ok, to in ((relay_right(pp), p + 1), (relay_left(pp), p - 1)):
                @pl.when(ok)
                def _():
                    co_wait(k, c * L + pp)
                    relay_copy(k, pp, to).start()

    def fwd_copy(k, pp):
        pos = c * L + pp
        return remote(co_buf.at[k, pos], co_buf.at[k, pos], co_fwd.at[k, pp], co_recv.at[k, pos], partner)

    def forward(k):
        for pp in range(L):
            @pl.when(pp != p)
            def _():
                @pl.when(jnp.logical_not(jnp.logical_or(relay_right(pp), relay_left(pp))))
                def _():
                    co_wait(k, c * L + pp)
                fwd_copy(k, pp).start()

    def s_copy(k, slot):
        lanes = pl.ds(pl.multiple_of(k * nw, nw), nw)
        return pltpu.make_async_copy(s_hbm.at[:, lanes], s_buf.at[slot], s_sem.at[slot])

    for d in range(1, L):
        t_line(d).start()
    for d in range(1, Q):
        t_peer(0, d).start()
    t_partner(0, 0).start()
    ahead = [0]

    def more_own(k):
        while ahead[0] < min(k, K):
            send_own(ahead[0])
            ahead[0] += 1

    def more(fn, k):
        if k < K:
            fn(k)

    more_own(3)
    s_copy(0, 0).start()
    t_buf[mypos, q] = t_ref[...]
    v_all[q] = v_ref[...]
    for k in range(K):
        co_buf[k, mypos] = co_ref[:, k * nw : (k + 1) * nw]
    for j in range(1, L):
        t_wait(c * L + (p + L - j) % L, q)
        for d in range(1, Q):
            t_peer(j, d).start()
        t_partner(j, 0).start()
    for d in range(1, Q):
        v_peer(d).start()
    more(relay, 0)
    more_own(4)
    for j in range(L):
        for d in range(1, Q):
            t_wait(c * L + (p + L - j) % L, (q + Q - d) % Q)
            t_partner(j, d).start()
    more(relay, 1)
    more(forward, 0)
    more_own(5)
    for pp in range(L):
        for qq in range(Q):
            t_wait((1 - c) * L + pp, qq)
    for pos in range(R):
        for qq in range(Q):
            for t in range(NT):
                hi, lo = split(t_buf[pos, qq, t])
                rows, lanes = slice(t * V + qq * vb, t * V + (qq + 1) * vb), slice(pos * cb, (pos + 1) * cb)
                t_hi[rows, lanes] = hi
                t_lo[rows, lanes] = lo

    def lanes_of(k):
        return pl.ds(pl.multiple_of(k * nw, nw), nw)

    def encode_half(k):
        for pp in range(L):
            co_wait(k, (1 - c) * L + pp)
        lanes = lanes_of(k)
        for pos in range(R):
            hi, lo = split(co_buf[k, pos])
            co_hi[pos * cb : (pos + 1) * cb, lanes] = hi
            co_lo[pos * cb : (pos + 1) * cb, lanes] = lo
        half = dot3(t_hi[...], t_lo[...], co_hi[:, lanes], co_lo[:, lanes])
        hi, lo = split(half)
        u_hi[:, lanes] = hi
        u_lo[:, lanes] = lo

    def project(slot, k, t):
        lanes = lanes_of(k)
        rows = pl.ds(pl.multiple_of(t * V, V), V)
        h_hi, h_lo = u_hi[rows, lanes], u_lo[rows, lanes]
        m = s_buf.shape[1]
        step = min(256, m)
        for r in range(0, m, step):
            block = slice(r, r + step)
            hi, lo = split(s_buf[slot, block] * dot3(vt_hi[block], vt_lo[block], h_hi, h_lo))
            p_hi[block] = hi
            p_lo[block] = lo
        step = min(256, V)
        for r in range(0, V, step):
            hi, lo = split(dot3(v_hi[r : r + step], v_lo[r : r + step], p_hi[...], p_lo[...]))
            rows = pl.ds(pl.multiple_of(t * V + r, step), step)
            u_hi[rows, lanes] = hi
            u_lo[rows, lanes] = lo

    more(relay, 2)
    more(forward, 1)
    more_own(6)
    encode_half(0)
    more(relay, 3)
    more(forward, 2)
    more_own(7)
    more(encode_half, 1)
    for d in range(1, Q):
        qq = (q + Q - d) % Q
        remote(v_all.at[qq], v_all.at[qq], v_send.at[0], v_recv.at[qq], partner).wait_recv()
    for qq in range(Q):
        hi, lo = split(v_all[qq])
        v_hi[qq * vb : (qq + 1) * vb, :] = hi
        v_lo[qq * vb : (qq + 1) * vb, :] = lo
    hi, lo = split(v_all[...].reshape(V, v_all.shape[2]).T)
    vt_hi[...] = hi
    vt_lo[...] = lo

    both = K // 2
    steps = both + NT * (K - both)

    def next_screened(i):
        @pl.when(i + 1 < steps)
        def _():
            later = jnp.where(i + 1 < both, i + 1, both + (i + 1 - both) % (K - both))
            s_copy(later, (i + 1) % 2).start()

    def stage(s, carry):
        @pl.when(s + 7 < K)
        def _():
            send_own(s + 7)

        @pl.when(s + 4 < K)
        def _():
            relay(s + 4)

        @pl.when(s + 3 < K)
        def _():
            forward(s + 3)

        @pl.when(s + 2 < K)
        def _():
            encode_half(s + 2)

        s_copy(s, s % 2).wait()
        next_screened(s)

        def one(t, carry):
            project(s % 2, s, t)
            return carry

        return lax.fori_loop(0, jnp.where(s < both, NT, 1), one, carry)

    lax.fori_loop(0, K, stage, 0)

    half_c = L * cb

    def decode(t, par):
        rows = slice(t * V, (t + 1) * V)
        cols = pl.ds(pl.multiple_of(par * half_c, half_c), half_c)
        return dot3(u_hi[rows, :], u_lo[rows, :], co_hi[cols, :], co_lo[cols, :], ((1,), (1,)))

    def p_copy(t):
        return remote(psend.at[t], precv.at[t], p_send.at[t], p_recv.at[t], partner)

    def x_copy(t, d):
        to = (q + d) % Q
        return remote(osum.at[t, to], xrecv.at[t, d], x_send.at[t, d], x_recv.at[t, d], peer(to))

    def z_copy(t, d):
        to = (p + d) % L
        return remote(zbuf.at[t, to], zrecv.at[t, d], z_send.at[t, d], z_recv.at[t, d], line(to))

    def to_partner(t):
        psend[t] = decode(t, 1 - c)
        p_copy(t).start()

    def to_peers(t):
        own = decode(t, c)
        p_copy(t).wait_recv()
        for qq in range(Q):
            osum[t, qq] = own[qq * vb : (qq + 1) * vb, :] + precv[t, qq * vb : (qq + 1) * vb, :]
        for d in range(Q - 1, 0, -1):
            x_copy(t, d).start()

    def to_line(t):
        total = osum[t, q]
        for d in range(Q - 1, 0, -1):
            x_copy(t, d).wait_recv()
            total = total + xrecv[t, d]
        for pp in range(L):
            zbuf[t, pp] = total[:, pp * cb : (pp + 1) * cb]
        for d in range(1, L):
            z_copy(t, d).start()

    def finish(t):
        final = zbuf[t, p]
        for d in range(1, L):
            z_copy(t, d).wait_recv()
            final = final + zrecv[t, d]
        out_ref[t] = final

    for t in range(NT):
        if t > 0:
            def later_stage(s, carry):
                i = both + t * (K - both) + s
                s_copy(both + s, i % 2).wait()
                next_screened(i)
                project(i % 2, both + s, t)
                return carry

            lax.fori_loop(0, K - both, later_stage, 0)
        to_partner(t)
        if t > 0:
            to_line(t - 1)
        to_peers(t)
    to_line(NT - 1)
    for t in range(NT):
        finish(t)

    for d in range(1, L):
        t_line(d).wait_send()
        for t in range(NT):
            z_copy(t, d).wait_send()
    for d in range(1, Q):
        v_peer(d).wait_send()
        for t in range(NT):
            x_copy(t, d).wait_send()
    for t in range(NT):
        p_copy(t).wait_send()
    for j in range(L):
        for d in range(1, Q):
            t_peer(j, d).wait_send()
        for d in range(Q):
            t_partner(j, d).wait_send()

    def drain(k, carry):
        for d, ok in own_cases():
            @pl.when(ok)
            def _():
                own_to(k, d).wait_send()
        own_partner(k).wait_send()
        for pp in range(L):
            for ok, to in ((relay_right(pp), p + 1), (relay_left(pp), p - 1)):
                @pl.when(ok)
                def _():
                    relay_copy(k, pp, to).wait_send()

            @pl.when(pp != p)
            def _():
                fwd_copy(k, pp).wait_send()
        return carry

    lax.fori_loop(0, K, drain, 0)


def body(R, Q, trials, valence_orb, conduction_orb, screened):
    NT, vb, cb = trials.shape
    m = valence_orb.shape[1]
    n = conduction_orb.shape[1]
    V, C, L = vb * Q, cb * R, R // 2
    nw = min(256, n)
    K = n // nw
    dma = pltpu.SemaphoreType.DMA
    vm = pl.BlockSpec(memory_space=pltpu.VMEM)
    return pl.pallas_call(
        functools.partial(kernel, R, Q, K),
        out_shape=jax.ShapeDtypeStruct((NT, vb, cb), F32),
        in_specs=[vm, vm, vm, pl.BlockSpec(memory_space=pl.ANY)],
        out_specs=vm,
        scratch_shapes=[
            pltpu.VMEM((R, Q, NT, vb, cb), F32),
            pltpu.VMEM((NT * V, C), BF16),
            pltpu.VMEM((NT * V, C), BF16),
            pltpu.VMEM((Q, vb, m), F32),
            pltpu.VMEM((V, m), BF16),
            pltpu.VMEM((V, m), BF16),
            pltpu.VMEM((m, V), BF16),
            pltpu.VMEM((m, V), BF16),
            pltpu.VMEM((K, R, cb, nw), F32),
            pltpu.VMEM((C, n), BF16),
            pltpu.VMEM((C, n), BF16),
            pltpu.VMEM((2, m, nw), F32),
            pltpu.VMEM((m, nw), BF16),
            pltpu.VMEM((m, nw), BF16),
            pltpu.VMEM((NT * V, n), BF16),
            pltpu.VMEM((NT * V, n), BF16),
            pltpu.VMEM((NT, V, L * cb), F32),
            pltpu.VMEM((NT, V, L * cb), F32),
            pltpu.VMEM((NT, Q, vb, L * cb), F32),
            pltpu.VMEM((NT, Q, vb, L * cb), F32),
            pltpu.VMEM((NT, L, vb, cb), F32),
            pltpu.VMEM((NT, L, vb, cb), F32),
            dma((R, Q)), dma((L,)), dma((L, Q)), dma((L, Q)),
            dma((Q,)), dma((Q,)),
            dma((K, R)), dma((K, 5)), dma((K, L)), dma((K, L)),
            dma((2,)),
            dma((NT,)), dma((NT,)), dma((NT, Q)), dma((NT, Q)), dma((NT, L)), dma((NT, L)),
        ],
        compiler_params=pltpu.CompilerParams(
            collective_id=0, has_side_effects=True, vmem_limit_bytes=67043328
        ),
    )(trials, valence_orb, conduction_orb, screened)


def solution(mesh):
    R, Q = mesh.shape["row"], mesh.shape["col"]
    placed = (P(None, "col", "row"), P("col", "row"), P("row", "col"), P("row", "col"))
    return jax.shard_map(
        functools.partial(body, R, Q), mesh=mesh, in_specs=placed,
        out_specs=P(None, "col", "row"), check_vma=False,
    )
```

```python
import functools

import jax
import jax.numpy as jnp
from jax import lax
from jax.experimental import pallas as pl
from jax.experimental.pallas import tpu as pltpu
from jax.sharding import PartitionSpec as P

F32 = jnp.float32
BF16 = jnp.bfloat16


def split(x):
    hi = x.astype(BF16)
    return hi, (x - hi.astype(F32)).astype(BF16)


def dot3(a_hi, a_lo, b_hi, b_lo, dims=((1,), (0,))):
    def one(a, b):
        return lax.dot_general(a, b, (dims, ((), ())), preferred_element_type=F32)

    return one(a_hi, b_hi) + (one(a_lo, b_hi) + one(a_hi, b_lo))


def kernel(
    R, Q, K,
    t_ref, v_ref, co_ref, s_hbm, out_ref,
    t_buf, t_hi, t_lo, v_all, v_hi, v_lo, vt_hi, vt_lo, co_buf, co_hi, co_lo, s_buf,
    p_hi, p_lo, u_hi, u_lo, psend, precv, osum, xrecv, zbuf, zrecv,
    t_recv, t_recv2, t_zs, t_xs, t_rs, t_ps, v_recv, v_send, co_recv, co_own, co_rel, co_fwd,
    s_sem, p_send, p_recv, x_send, x_recv, z_send, z_recv,
):
    NT, vb, cb = t_ref.shape
    V = vb * Q
    L = R // 2
    nw = co_buf.shape[3]
    row, q = lax.axis_index("row"), lax.axis_index("col")
    p, c = row // 2, row % 2
    mypos = c * L + p
    partner = (p * 2 + (1 - c), q)

    def line(pp):
        return (pp * 2 + c, q)

    def peer(qq):
        return (row, qq)

    def remote(src, dst, ss, rs, dev):
        return pltpu.make_async_remote_copy(
            src_ref=src, dst_ref=dst, send_sem=ss, recv_sem=rs,
            device_id=dev, device_id_type=pl.DeviceIdType.MESH,
        )

    barrier = pltpu.get_barrier_semaphore()
    others = [partner]
    others += [line((p + d) % L) for d in range(1, L)]
    others += [peer((q + d) % Q) for d in range(1, Q)]
    for dev in others:
        pl.semaphore_signal(barrier, inc=1, device_id=dev, device_id_type=pl.DeviceIdType.MESH)
    pl.semaphore_wait(barrier, len(others))

    def t_line(d):
        return remote(t_ref, t_buf.at[mypos, q], t_zs.at[d], t_recv.at[mypos, q], line((p + d) % L))

    square = Q == 4 and vb % 16 == 0
    sides = (q + 1 - 2 * (q % 2), (q + 2) % 4) if square else ()
    corner = 3 - q
    half_rows = [pl.ds(i * (vb // 2), vb // 2) for i in range(2)]

    def t_pos(j):
        return c * L + (p + L - j) % L

    def t_peer(j, d):
        pos = t_pos(j)
        src = t_ref if j == 0 else t_buf.at[pos, q]
        to = sides[d - 1] if square else (q + d) % Q
        return remote(src, t_buf.at[pos, q], t_xs.at[j, d], t_recv.at[pos, q], peer(to))

    def t_relay(j, i):
        part = t_buf.at[t_pos(j), sides[i], :, half_rows[i]]
        sem = t_recv if i == 0 else t_recv2
        return remote(part, part, t_rs.at[j, i], sem.at[t_pos(j), sides[i]], peer(sides[1 - i]))

    def t_corner_wait(j):
        for i in range(2):
            part = t_buf.at[t_pos(j), corner, :, half_rows[i]]
            sem = t_recv if i == 0 else t_recv2
            remote(part, part, t_zs.at[0], sem.at[t_pos(j), corner], partner).wait_recv()

    peers = range(1, 3 if square else Q)

    def t_partner(j, d):
        pos = c * L + (p + L - j) % L
        qq = (q, *sides, corner)[d] if square else (q + Q - d) % Q
        src = t_ref if (j == 0 and d == 0) else t_buf.at[pos, qq]
        return remote(src, t_buf.at[pos, qq], t_ps.at[j, d], t_recv.at[pos, qq], partner)

    def t_wait(pos, qq):
        remote(t_buf.at[pos, qq], t_buf.at[pos, qq], t_zs.at[0], t_recv.at[pos, qq], partner).wait_recv()

    def v_peer(d):
        return remote(v_ref, v_all.at[q], v_send.at[d, 0], v_recv.at[q, 0], peer((q + d) % Q))

    def v_side(i, part):
        rows = half_rows[part]
        return remote(
            v_ref.at[rows], v_all.at[q, rows], v_send.at[i, part], v_recv.at[q, part], peer(sides[i])
        )

    def v_relay(i):
        part = v_all.at[sides[i], half_rows[i]]
        return remote(part, part, v_send.at[2, i], v_recv.at[sides[i], i], peer(sides[1 - i]))

    def v_wait(qq, part):
        rows = v_all.at[qq, half_rows[part]]
        remote(rows, rows, v_send.at[0, 0], v_recv.at[qq, part], partner).wait_recv()

    def own_to(k, d):
        lanes = pl.ds(pl.multiple_of(k * nw, nw), nw)
        sign = 1 if d > 0 else -1
        return remote(
            co_ref.at[:, lanes], co_buf.at[k, mypos],
            co_own.at[k, abs(d) - 1 + (2 if sign < 0 else 0)], co_recv.at[k, mypos],
            line(jnp.clip(p + d, 0, L - 1)),
        )

    def own_partner(k):
        lanes = pl.ds(pl.multiple_of(k * nw, nw), nw)
        return remote(
            co_ref.at[:, lanes], co_buf.at[k, mypos], co_own.at[k, 4], co_recv.at[k, mypos], partner
        )

    def own_cases():
        for d in (1, 2):
            if d < L:
                yield d, p + d <= L - 1
                yield -d, p - d >= 0

    def send_own(k):
        for d, ok in own_cases():
            @pl.when(ok)
            def _():
                own_to(k, d).start()
        own_partner(k).start()

    def relay_right(pp):
        return jnp.logical_and(p - pp >= 2, p < L - 1)

    def relay_left(pp):
        return jnp.logical_and(pp - p >= 2, p > 0)

    def relay_copy(k, pp, to):
        pos = c * L + pp
        return remote(
            co_buf.at[k, pos], co_buf.at[k, pos], co_rel.at[k, pp], co_recv.at[k, pos],
            line(jnp.clip(to, 0, L - 1)),
        )

    def co_wait(k, pos):
        remote(co_buf.at[k, pos], co_buf.at[k, pos], co_own.at[k, 4], co_recv.at[k, pos], partner).wait_recv()

    def relay(k):
        for pp in range(L):
            for ok, to in ((relay_right(pp), p + 1), (relay_left(pp), p - 1)):
                @pl.when(ok)
                def _():
                    co_wait(k, c * L + pp)
                    relay_copy(k, pp, to).start()

    def fwd_copy(k, pp):
        pos = c * L + pp
        return remote(co_buf.at[k, pos], co_buf.at[k, pos], co_fwd.at[k, pp], co_recv.at[k, pos], partner)

    def forward(k):
        for pp in range(L):
            @pl.when(pp != p)
            def _():
                @pl.when(jnp.logical_not(jnp.logical_or(relay_right(pp), relay_left(pp))))
                def _():
                    co_wait(k, c * L + pp)
                fwd_copy(k, pp).start()

    def s_copy(k, slot):
        lanes = pl.ds(pl.multiple_of(k * nw, nw), nw)
        return pltpu.make_async_copy(s_hbm.at[:, lanes], s_buf.at[slot], s_sem.at[slot])

    for d in range(1, L):
        t_line(d).start()
    for d in peers:
        t_peer(0, d).start()
    t_partner(0, 0).start()
    if square:
        for i in range(2):
            v_side(i, i).start()
    ahead = [0]

    def more_own(k):
        while ahead[0] < min(k, K):
            send_own(ahead[0])
            ahead[0] += 1

    def more(fn, k):
        if k < K:
            fn(k)

    more_own(3)
    s_copy(0, 0).start()
    t_buf[mypos, q] = t_ref[...]
    v_all[q] = v_ref[...]
    for k in range(K):
        co_buf[k, mypos] = co_ref[:, k * nw : (k + 1) * nw]
    for j in range(1, L):
        t_wait(t_pos(j), q)
        for d in peers:
            t_peer(j, d).start()
        t_partner(j, 0).start()
    if square:
        for i in range(2):
            v_side(i, 1 - i).start()
        more(relay, 0)
        more_own(4)
        for j in range(L):
            for i in range(2):
                t_wait(t_pos(j), sides[i])
                t_relay(j, i).start()
                t_partner(j, 1 + i).start()
        for i in range(2):
            v_wait(sides[i], i)
            v_relay(i).start()
        for j in range(L):
            t_corner_wait(j)
            t_partner(j, 3).start()
    else:
        for d in range(1, Q):
            v_peer(d).start()
        more(relay, 0)
        more_own(4)
        for j in range(L):
            for d in range(1, Q):
                t_wait(t_pos(j), (q + Q - d) % Q)
                t_partner(j, d).start()
    more(relay, 1)
    more(forward, 0)
    more_own(5)
    for pp in range(L):
        for qq in range(Q):
            t_wait((1 - c) * L + pp, qq)
    for pos in range(R):
        for qq in range(Q):
            for t in range(NT):
                hi, lo = split(t_buf[pos, qq, t])
                rows, lanes = slice(t * V + qq * vb, t * V + (qq + 1) * vb), slice(pos * cb, (pos + 1) * cb)
                t_hi[rows, lanes] = hi
                t_lo[rows, lanes] = lo

    def lanes_of(k):
        return pl.ds(pl.multiple_of(k * nw, nw), nw)

    def encode_half(k):
        for pp in range(L):
            co_wait(k, (1 - c) * L + pp)
        lanes = lanes_of(k)
        for pos in range(R):
            hi, lo = split(co_buf[k, pos])
            co_hi[pos * cb : (pos + 1) * cb, lanes] = hi
            co_lo[pos * cb : (pos + 1) * cb, lanes] = lo
        half = dot3(t_hi[...], t_lo[...], co_hi[:, lanes], co_lo[:, lanes])
        hi, lo = split(half)
        u_hi[:, lanes] = hi
        u_lo[:, lanes] = lo

    def project(slot, k, t):
        lanes = lanes_of(k)
        rows = pl.ds(pl.multiple_of(t * V, V), V)
        h_hi, h_lo = u_hi[rows, lanes], u_lo[rows, lanes]
        m = s_buf.shape[1]
        step = min(256, m)
        for r in range(0, m, step):
            block = slice(r, r + step)
            hi, lo = split(s_buf[slot, block] * dot3(vt_hi[block], vt_lo[block], h_hi, h_lo))
            p_hi[block] = hi
            p_lo[block] = lo
        step = min(256, V)
        for r in range(0, V, step):
            hi, lo = split(dot3(v_hi[r : r + step], v_lo[r : r + step], p_hi[...], p_lo[...]))
            rows = pl.ds(pl.multiple_of(t * V + r, step), step)
            u_hi[rows, lanes] = hi
            u_lo[rows, lanes] = lo

    more_own(6)
    encode_half(0)
    more(relay, 2)
    more(forward, 1)
    more_own(7)
    if square:
        for i in range(2):
            v_wait(sides[i], 1 - i)
        for i in range(2):
            v_wait(corner, i)
    else:
        for d in range(1, Q):
            qq = (q + Q - d) % Q
            remote(v_all.at[qq], v_all.at[qq], v_send.at[0, 0], v_recv.at[qq, 0], partner).wait_recv()
    for qq in range(Q):
        hi, lo = split(v_all[qq])
        v_hi[qq * vb : (qq + 1) * vb, :] = hi
        v_lo[qq * vb : (qq + 1) * vb, :] = lo
    hi, lo = split(v_all[...].reshape(V, v_all.shape[2]).T)
    vt_hi[...] = hi
    vt_lo[...] = lo

    both = K // 2
    steps = both + NT * (K - both)

    def next_screened(i):
        @pl.when(i + 1 < steps)
        def _():
            later = jnp.where(i + 1 < both, i + 1, both + (i + 1 - both) % (K - both))
            s_copy(later, (i + 1) % 2).start()

    def stage(s, carry):
        @pl.when(s + 7 < K)
        def _():
            send_own(s + 7)

        @pl.when(s + 3 < K)
        def _():
            relay(s + 3)

        @pl.when(s + 2 < K)
        def _():
            forward(s + 2)

        @pl.when(s + 1 < K)
        def _():
            encode_half(s + 1)

        s_copy(s, s % 2).wait()
        next_screened(s)

        def one(t, carry):
            project(s % 2, s, t)
            return carry

        return lax.fori_loop(0, jnp.where(s < both, NT, 1), one, carry)

    lax.fori_loop(0, K, stage, 0)

    half_c = L * cb

    def decode(t, par):
        rows = slice(t * V, (t + 1) * V)
        cols = pl.ds(pl.multiple_of(par * half_c, half_c), half_c)
        return dot3(u_hi[rows, :], u_lo[rows, :], co_hi[cols, :], co_lo[cols, :], ((1,), (1,)))

    def p_copy(t):
        return remote(psend.at[t], precv.at[t], p_send.at[t], p_recv.at[t], partner)

    def x_copy(t, d):
        to = (q + d) % Q
        return remote(osum.at[t, to], xrecv.at[t, d], x_send.at[t, d], x_recv.at[t, d], peer(to))

    def z_copy(t, d):
        to = (p + d) % L
        return remote(zbuf.at[t, to], zrecv.at[t, d], z_send.at[t, d], z_recv.at[t, d], line(to))

    def to_partner(t):
        psend[t] = decode(t, 1 - c)
        p_copy(t).start()

    def to_peers(t):
        own = decode(t, c)
        p_copy(t).wait_recv()
        for qq in range(Q):
            osum[t, qq] = own[qq * vb : (qq + 1) * vb, :] + precv[t, qq * vb : (qq + 1) * vb, :]
        for d in range(Q - 1, 0, -1):
            x_copy(t, d).start()

    def to_line(t):
        total = osum[t, q]
        for d in range(Q - 1, 0, -1):
            x_copy(t, d).wait_recv()
            total = total + xrecv[t, d]
        for pp in range(L):
            zbuf[t, pp] = total[:, pp * cb : (pp + 1) * cb]
        for d in range(1, L):
            z_copy(t, d).start()

    def finish(t):
        final = zbuf[t, p]
        for d in range(1, L):
            z_copy(t, d).wait_recv()
            final = final + zrecv[t, d]
        out_ref[t] = final

    for t in range(NT):
        if t > 0:
            def later_stage(s, carry):
                i = both + t * (K - both) + s
                s_copy(both + s, i % 2).wait()
                next_screened(i)
                project(i % 2, both + s, t)
                return carry

            lax.fori_loop(0, K - both, later_stage, 0)
        to_partner(t)
        if t > 0:
            to_line(t - 1)
        to_peers(t)
    to_line(NT - 1)
    for t in range(NT):
        finish(t)

    for d in range(1, L):
        t_line(d).wait_send()
        for t in range(NT):
            z_copy(t, d).wait_send()
    for d in range(1, Q):
        for t in range(NT):
            x_copy(t, d).wait_send()
    if square:
        for i in range(2):
            v_relay(i).wait_send()
            for part in range(2):
                v_side(i, part).wait_send()
    else:
        for d in range(1, Q):
            v_peer(d).wait_send()
    for t in range(NT):
        p_copy(t).wait_send()
    for j in range(L):
        for d in peers:
            t_peer(j, d).wait_send()
        if square:
            for i in range(2):
                t_relay(j, i).wait_send()
        for d in range(Q):
            t_partner(j, d).wait_send()

    def drain(k, carry):
        for d, ok in own_cases():
            @pl.when(ok)
            def _():
                own_to(k, d).wait_send()
        own_partner(k).wait_send()
        for pp in range(L):
            for ok, to in ((relay_right(pp), p + 1), (relay_left(pp), p - 1)):
                @pl.when(ok)
                def _():
                    relay_copy(k, pp, to).wait_send()

            @pl.when(pp != p)
            def _():
                fwd_copy(k, pp).wait_send()
        return carry

    lax.fori_loop(0, K, drain, 0)


def body(R, Q, trials, valence_orb, conduction_orb, screened):
    NT, vb, cb = trials.shape
    m = valence_orb.shape[1]
    n = conduction_orb.shape[1]
    V, C, L = vb * Q, cb * R, R // 2
    nw = min(256, n)
    K = n // nw
    dma = pltpu.SemaphoreType.DMA
    vm = pl.BlockSpec(memory_space=pltpu.VMEM)
    return pl.pallas_call(
        functools.partial(kernel, R, Q, K),
        out_shape=jax.ShapeDtypeStruct((NT, vb, cb), F32),
        in_specs=[vm, vm, vm, pl.BlockSpec(memory_space=pl.ANY)],
        out_specs=vm,
        scratch_shapes=[
            pltpu.VMEM((R, Q, NT, vb, cb), F32),
            pltpu.VMEM((NT * V, C), BF16),
            pltpu.VMEM((NT * V, C), BF16),
            pltpu.VMEM((Q, vb, m), F32),
            pltpu.VMEM((V, m), BF16),
            pltpu.VMEM((V, m), BF16),
            pltpu.VMEM((m, V), BF16),
            pltpu.VMEM((m, V), BF16),
            pltpu.VMEM((K, R, cb, nw), F32),
            pltpu.VMEM((C, n), BF16),
            pltpu.VMEM((C, n), BF16),
            pltpu.VMEM((2, m, nw), F32),
            pltpu.VMEM((m, nw), BF16),
            pltpu.VMEM((m, nw), BF16),
            pltpu.VMEM((NT * V, n), BF16),
            pltpu.VMEM((NT * V, n), BF16),
            pltpu.VMEM((NT, V, L * cb), F32),
            pltpu.VMEM((NT, V, L * cb), F32),
            pltpu.VMEM((NT, Q, vb, L * cb), F32),
            pltpu.VMEM((NT, Q, vb, L * cb), F32),
            pltpu.VMEM((NT, L, vb, cb), F32),
            pltpu.VMEM((NT, L, vb, cb), F32),
            dma((R, Q)), dma((R, Q)), dma((L,)), dma((L, Q)), dma((L, 2)), dma((L, Q)),
            dma((Q, 2)), dma((Q, 2)),
            dma((K, R)), dma((K, 5)), dma((K, L)), dma((K, L)),
            dma((2,)),
            dma((NT,)), dma((NT,)), dma((NT, Q)), dma((NT, Q)), dma((NT, L)), dma((NT, L)),
        ],
        compiler_params=pltpu.CompilerParams(
            collective_id=0, has_side_effects=True, vmem_limit_bytes=67043328
        ),
    )(trials, valence_orb, conduction_orb, screened)


def solution(mesh):
    R, Q = mesh.shape["row"], mesh.shape["col"]
    placed = (P(None, "col", "row"), P("col", "row"), P("row", "col"), P("row", "col"))
    return jax.shard_map(
        functools.partial(body, R, Q), mesh=mesh, in_specs=placed,
        out_specs=P(None, "col", "row"), check_vma=False,
    )
```

```python
import functools

import jax
import jax.numpy as jnp
from jax import lax
from jax.experimental import pallas as pl
from jax.experimental.pallas import tpu as pltpu
from jax.sharding import PartitionSpec as P

F32 = jnp.float32
BF16 = jnp.bfloat16


def split(x):
    hi = x.astype(BF16)
    return hi, (x - hi.astype(F32)).astype(BF16)


def dot3(a_hi, a_lo, b_hi, b_lo, dims=((1,), (0,))):
    def one(a, b):
        return lax.dot_general(a, b, (dims, ((), ())), preferred_element_type=F32)

    return one(a_hi, b_hi) + (one(a_lo, b_hi) + one(a_hi, b_lo))


def kernel(
    R, Q, K,
    t_ref, v_ref, co_ref, s_hbm, out_ref,
    t_buf, t_hi, t_lo, v_all, v_hi, v_lo, vt_hi, vt_lo, co_buf, co_hi, co_lo, s_buf,
    p_hi, p_lo, u_hi, u_lo, psend, precv, osum, xrecv, zbuf, zrecv,
    t_recv, t_recv2, t_zs, t_xs, t_rs, t_ps, v_recv, v_send, co_recv, co_own, co_rel, co_fwd,
    s_sem, p_send, p_recv, x_send, x_recv, z_send, z_recv,
):
    NT, vb, cb = t_ref.shape
    V = vb * Q
    L = R // 2
    nw = co_buf.shape[3]
    row, q = lax.axis_index("row"), lax.axis_index("col")
    p, c = row // 2, row % 2
    mypos = c * L + p
    partner = (p * 2 + (1 - c), q)

    def line(pp):
        return (pp * 2 + c, q)

    def peer(qq):
        return (row, qq)

    def remote(src, dst, ss, rs, dev):
        return pltpu.make_async_remote_copy(
            src_ref=src, dst_ref=dst, send_sem=ss, recv_sem=rs,
            device_id=dev, device_id_type=pl.DeviceIdType.MESH,
        )

    barrier = pltpu.get_barrier_semaphore()
    others = [partner]
    others += [line((p + d) % L) for d in range(1, L)]
    others += [peer((q + d) % Q) for d in range(1, Q)]
    for dev in others:
        pl.semaphore_signal(barrier, inc=1, device_id=dev, device_id_type=pl.DeviceIdType.MESH)
    pl.semaphore_wait(barrier, len(others))

    def t_line(d):
        return remote(t_ref, t_buf.at[mypos, q], t_zs.at[d], t_recv.at[mypos, q], line((p + d) % L))

    square = Q == 4 and vb % 16 == 0
    sides = (q + 1 - 2 * (q % 2), (q + 2) % 4) if square else ()
    corner = 3 - q
    half_rows = [pl.ds(i * (vb // 2), vb // 2) for i in range(2)]

    def t_pos(j):
        return c * L + (p + L - j) % L

    def t_peer(j, d):
        pos = t_pos(j)
        src = t_ref if j == 0 else t_buf.at[pos, q]
        to = sides[d - 1] if square else (q + d) % Q
        return remote(src, t_buf.at[pos, q], t_xs.at[j, d], t_recv.at[pos, q], peer(to))

    def t_relay(j, i):
        part = t_buf.at[t_pos(j), sides[i], :, half_rows[i]]
        sem = t_recv if i == 0 else t_recv2
        return remote(part, part, t_rs.at[j, i], sem.at[t_pos(j), sides[i]], peer(sides[1 - i]))

    def t_corner_wait(j):
        for i in range(2):
            part = t_buf.at[t_pos(j), corner, :, half_rows[i]]
            sem = t_recv if i == 0 else t_recv2
            remote(part, part, t_zs.at[0], sem.at[t_pos(j), corner], partner).wait_recv()

    peers = range(1, 3 if square else Q)

    def t_partner(j, d):
        pos = c * L + (p + L - j) % L
        qq = (q, *sides, corner)[d] if square else (q + Q - d) % Q
        src = t_ref if (j == 0 and d == 0) else t_buf.at[pos, qq]
        return remote(src, t_buf.at[pos, qq], t_ps.at[j, d], t_recv.at[pos, qq], partner)

    def t_wait(pos, qq):
        remote(t_buf.at[pos, qq], t_buf.at[pos, qq], t_zs.at[0], t_recv.at[pos, qq], partner).wait_recv()

    def v_peer(d):
        return remote(v_ref, v_all.at[q], v_send.at[d, 0], v_recv.at[q, 0], peer((q + d) % Q))

    def v_side(i, part):
        rows = half_rows[part]
        return remote(
            v_ref.at[rows], v_all.at[q, rows], v_send.at[i, part], v_recv.at[q, part], peer(sides[i])
        )

    def v_relay(i):
        part = v_all.at[sides[i], half_rows[i]]
        return remote(part, part, v_send.at[2, i], v_recv.at[sides[i], i], peer(sides[1 - i]))

    def v_wait(qq, part):
        rows = v_all.at[qq, half_rows[part]]
        remote(rows, rows, v_send.at[0, 0], v_recv.at[qq, part], partner).wait_recv()

    def own_to(k, d):
        lanes = pl.ds(pl.multiple_of(k * nw, nw), nw)
        sign = 1 if d > 0 else -1
        return remote(
            co_ref.at[:, lanes], co_buf.at[k, mypos],
            co_own.at[k, abs(d) - 1 + (2 if sign < 0 else 0)], co_recv.at[k, mypos],
            line(jnp.clip(p + d, 0, L - 1)),
        )

    def own_partner(k):
        lanes = pl.ds(pl.multiple_of(k * nw, nw), nw)
        return remote(
            co_ref.at[:, lanes], co_buf.at[k, mypos], co_own.at[k, 4], co_recv.at[k, mypos], partner
        )

    def own_cases():
        for d in (1, 2):
            if d < L:
                yield d, p + d <= L - 1
                yield -d, p - d >= 0

    def send_own(k):
        for d, ok in own_cases():
            @pl.when(ok)
            def _():
                own_to(k, d).start()
        own_partner(k).start()

    def relay_right(pp):
        return jnp.logical_and(p - pp >= 2, p < L - 1)

    def relay_left(pp):
        return jnp.logical_and(pp - p >= 2, p > 0)

    def relay_copy(k, pp, to):
        pos = c * L + pp
        return remote(
            co_buf.at[k, pos], co_buf.at[k, pos], co_rel.at[k, pp], co_recv.at[k, pos],
            line(jnp.clip(to, 0, L - 1)),
        )

    def co_wait(k, pos):
        remote(co_buf.at[k, pos], co_buf.at[k, pos], co_own.at[k, 4], co_recv.at[k, pos], partner).wait_recv()

    def relay(k):
        for pp in range(L):
            for ok, to in ((relay_right(pp), p + 1), (relay_left(pp), p - 1)):
                @pl.when(ok)
                def _():
                    co_wait(k, c * L + pp)
                    relay_copy(k, pp, to).start()

    def fwd_copy(k, pp):
        pos = c * L + pp
        return remote(co_buf.at[k, pos], co_buf.at[k, pos], co_fwd.at[k, pp], co_recv.at[k, pos], partner)

    def forward(k):
        for pp in range(L):
            @pl.when(pp != p)
            def _():
                @pl.when(jnp.logical_not(jnp.logical_or(relay_right(pp), relay_left(pp))))
                def _():
                    co_wait(k, c * L + pp)
                fwd_copy(k, pp).start()

    def s_copy(k, slot):
        lanes = pl.ds(pl.multiple_of(k * nw, nw), nw)
        return pltpu.make_async_copy(s_hbm.at[:, lanes], s_buf.at[slot], s_sem.at[slot])

    for d in range(1, L):
        t_line(d).start()
    for d in peers:
        t_peer(0, d).start()
    t_partner(0, 0).start()
    if square:
        for i in range(2):
            v_side(i, i).start()
    ahead = [0]

    def more_own(k):
        while ahead[0] < min(k, K):
            send_own(ahead[0])
            ahead[0] += 1

    def more(fn, k):
        if k < K:
            fn(k)

    more_own(3)
    s_copy(0, 0).start()
    t_buf[mypos, q] = t_ref[...]
    v_all[q] = v_ref[...]
    for k in range(K):
        co_buf[k, mypos] = co_ref[:, k * nw : (k + 1) * nw]
    for j in range(1, L):
        t_wait(t_pos(j), q)
        for d in peers:
            t_peer(j, d).start()
        t_partner(j, 0).start()
    if square:
        for i in range(2):
            v_side(i, 1 - i).start()
        more(relay, 0)
        more_own(4)
        for j in range(L):
            for i in range(2):
                t_wait(t_pos(j), sides[i])
                t_relay(j, i).start()
                t_partner(j, 1 + i).start()
        for i in range(2):
            v_wait(sides[i], i)
            v_relay(i).start()
        for j in range(L):
            t_corner_wait(j)
            t_partner(j, 3).start()
    else:
        for d in range(1, Q):
            v_peer(d).start()
        more(relay, 0)
        more_own(4)
        for j in range(L):
            for d in range(1, Q):
                t_wait(t_pos(j), (q + Q - d) % Q)
                t_partner(j, d).start()
    more(relay, 1)
    more(forward, 0)
    more_own(5)
    for pp in range(L):
        for qq in range(Q):
            t_wait((1 - c) * L + pp, qq)
    for pos in range(R):
        for qq in range(Q):
            for t in range(NT):
                hi, lo = split(t_buf[pos, qq, t])
                rows, lanes = slice(t * V + qq * vb, t * V + (qq + 1) * vb), slice(pos * cb, (pos + 1) * cb)
                t_hi[rows, lanes] = hi
                t_lo[rows, lanes] = lo

    def lanes_of(k):
        return pl.ds(pl.multiple_of(k * nw, nw), nw)

    def encode_half(k):
        for pp in range(L):
            co_wait(k, (1 - c) * L + pp)
        lanes = lanes_of(k)
        for pos in range(R):
            hi, lo = split(co_buf[k, pos])
            co_hi[pos * cb : (pos + 1) * cb, lanes] = hi
            co_lo[pos * cb : (pos + 1) * cb, lanes] = lo
        half = dot3(t_hi[...], t_lo[...], co_hi[:, lanes], co_lo[:, lanes])
        hi, lo = split(half)
        u_hi[:, lanes] = hi
        u_lo[:, lanes] = lo

    def project(slot, k, t):
        lanes = lanes_of(k)
        rows = pl.ds(pl.multiple_of(t * V, V), V)
        h_hi, h_lo = u_hi[rows, lanes], u_lo[rows, lanes]
        m = s_buf.shape[1]
        step = min(256, m)
        for r in range(0, m, step):
            block = slice(r, r + step)
            hi, lo = split(s_buf[slot, block] * dot3(vt_hi[block], vt_lo[block], h_hi, h_lo))
            p_hi[block] = hi
            p_lo[block] = lo
        step = min(256, V)
        for r in range(0, V, step):
            hi, lo = split(dot3(v_hi[r : r + step], v_lo[r : r + step], p_hi[...], p_lo[...]))
            rows = pl.ds(pl.multiple_of(t * V + r, step), step)
            u_hi[rows, lanes] = hi
            u_lo[rows, lanes] = lo

    more_own(6)
    encode_half(0)
    more(relay, 2)
    more(forward, 1)
    more_own(7)
    if square:
        for i in range(2):
            v_wait(sides[i], 1 - i)
        for i in range(2):
            v_wait(corner, i)
    else:
        for d in range(1, Q):
            qq = (q + Q - d) % Q
            remote(v_all.at[qq], v_all.at[qq], v_send.at[0, 0], v_recv.at[qq, 0], partner).wait_recv()
    for qq in range(Q):
        hi, lo = split(v_all[qq])
        v_hi[qq * vb : (qq + 1) * vb, :] = hi
        v_lo[qq * vb : (qq + 1) * vb, :] = lo
    hi, lo = split(v_all[...].reshape(V, v_all.shape[2]).T)
    vt_hi[...] = hi
    vt_lo[...] = lo

    both = K // 2
    steps = both + NT * (K - both)

    def next_screened(i):
        @pl.when(i + 1 < steps)
        def _():
            later = jnp.where(i + 1 < both, i + 1, both + (i + 1 - both) % (K - both))
            s_copy(later, (i + 1) % 2).start()

    def stage(s, carry):
        @pl.when(s + 7 < K)
        def _():
            send_own(s + 7)

        @pl.when(s + 3 < K)
        def _():
            relay(s + 3)

        @pl.when(s + 2 < K)
        def _():
            forward(s + 2)

        @pl.when(s + 1 < K)
        def _():
            encode_half(s + 1)

        s_copy(s, s % 2).wait()
        next_screened(s)

        def one(t, carry):
            project(s % 2, s, t)
            return carry

        return lax.fori_loop(0, jnp.where(s < both, NT, 1), one, carry)

    lax.fori_loop(0, K, stage, 0)

    half_c = L * cb

    parts = 2 if Q % 2 == 0 else 1
    pq = Q // parts
    pv = V // parts

    def side_of(h):
        return (q // pq + parts - 1 - h) % parts

    def part_rows(h):
        return pl.ds(pl.multiple_of(side_of(h) * pv, pv), pv)

    def decode(t, par, h):
        rows = pl.ds(pl.multiple_of(t * V + side_of(h) * pv, pv), pv)
        cols = pl.ds(pl.multiple_of(par * half_c, half_c), half_c)
        return dot3(u_hi[rows, :], u_lo[rows, :], co_hi[cols, :], co_lo[cols, :], ((1,), (1,)))

    def p_copy(t, h):
        rows = part_rows(h)
        return remote(psend.at[t, rows], precv.at[t, rows], p_send.at[t, h], p_recv.at[t, h], partner)

    def peer_at(h, i):
        return side_of(h) * pq + (q + i) % pq

    def x_copy(t, h, i):
        to = peer_at(h, i)
        e = h * pq + i
        return remote(osum.at[t, to], xrecv.at[t, e], x_send.at[t, e], x_recv.at[t, e], peer(to))

    hops = [(h, i) for h in range(parts) for i in range(pq) if h < parts - 1 or i > 0]

    def x_wait(t, h, i):
        e = h * pq + i
        remote(xrecv.at[t, e], xrecv.at[t, e], x_send.at[t, e], x_recv.at[t, e], partner).wait_recv()

    def z_copy(t, d):
        to = (p + d) % L
        return remote(zbuf.at[t, to], zrecv.at[t, d], z_send.at[t, d], z_recv.at[t, d], line(to))

    def to_partner(t, h):
        psend[t, part_rows(h)] = decode(t, 1 - c, h)
        p_copy(t, h).start()

    def to_peers(t, h):
        own = decode(t, c, h)
        p_copy(t, h).wait_recv()
        for i in range(pq):
            qq = side_of(h) * pq + i
            rows = pl.ds(pl.multiple_of(qq * vb, vb), vb)
            osum[t, qq] = own[i * vb : (i + 1) * vb, :] + precv[t, rows, :]
        for g, i in hops:
            if g == h:
                x_copy(t, g, i).start()

    def to_line(t):
        total = osum[t, q]
        for h, i in hops:
            x_wait(t, h, i)
            total = total + xrecv[t, h * pq + i]
        for pp in range(L):
            zbuf[t, pp] = total[:, pp * cb : (pp + 1) * cb]
        for d in range(1, L):
            z_copy(t, d).start()

    def finish(t):
        final = zbuf[t, p]
        for d in range(1, L):
            z_copy(t, d).wait_recv()
            final = final + zrecv[t, d]
        out_ref[t] = final

    for t in range(NT):
        if t > 0:
            def later_stage(s, carry):
                i = both + t * (K - both) + s
                s_copy(both + s, i % 2).wait()
                next_screened(i)
                project(i % 2, both + s, t)
                return carry

            lax.fori_loop(0, K - both, later_stage, 0)
        to_partner(t, 0)
        if t > 0:
            to_line(t - 1)
        for h in range(parts):
            to_peers(t, h)
            if h + 1 < parts:
                to_partner(t, h + 1)
    to_line(NT - 1)
    for t in range(NT):
        finish(t)

    for d in range(1, L):
        t_line(d).wait_send()
        for t in range(NT):
            z_copy(t, d).wait_send()
    for t in range(NT):
        for h, i in hops:
            x_copy(t, h, i).wait_send()
    if square:
        for i in range(2):
            v_relay(i).wait_send()
            for part in range(2):
                v_side(i, part).wait_send()
    else:
        for d in range(1, Q):
            v_peer(d).wait_send()
    for t in range(NT):
        for h in range(parts):
            p_copy(t, h).wait_send()
    for j in range(L):
        for d in peers:
            t_peer(j, d).wait_send()
        if square:
            for i in range(2):
                t_relay(j, i).wait_send()
        for d in range(Q):
            t_partner(j, d).wait_send()

    def drain(k, carry):
        for d, ok in own_cases():
            @pl.when(ok)
            def _():
                own_to(k, d).wait_send()
        own_partner(k).wait_send()
        for pp in range(L):
            for ok, to in ((relay_right(pp), p + 1), (relay_left(pp), p - 1)):
                @pl.when(ok)
                def _():
                    relay_copy(k, pp, to).wait_send()

            @pl.when(pp != p)
            def _():
                fwd_copy(k, pp).wait_send()
        return carry

    lax.fori_loop(0, K, drain, 0)


def body(R, Q, trials, valence_orb, conduction_orb, screened):
    NT, vb, cb = trials.shape
    m = valence_orb.shape[1]
    n = conduction_orb.shape[1]
    V, C, L = vb * Q, cb * R, R // 2
    nw = min(256, n)
    K = n // nw
    dma = pltpu.SemaphoreType.DMA
    vm = pl.BlockSpec(memory_space=pltpu.VMEM)
    return pl.pallas_call(
        functools.partial(kernel, R, Q, K),
        out_shape=jax.ShapeDtypeStruct((NT, vb, cb), F32),
        in_specs=[vm, vm, vm, pl.BlockSpec(memory_space=pl.ANY)],
        out_specs=vm,
        scratch_shapes=[
            pltpu.VMEM((R, Q, NT, vb, cb), F32),
            pltpu.VMEM((NT * V, C), BF16),
            pltpu.VMEM((NT * V, C), BF16),
            pltpu.VMEM((Q, vb, m), F32),
            pltpu.VMEM((V, m), BF16),
            pltpu.VMEM((V, m), BF16),
            pltpu.VMEM((m, V), BF16),
            pltpu.VMEM((m, V), BF16),
            pltpu.VMEM((K, R, cb, nw), F32),
            pltpu.VMEM((C, n), BF16),
            pltpu.VMEM((C, n), BF16),
            pltpu.VMEM((2, m, nw), F32),
            pltpu.VMEM((m, nw), BF16),
            pltpu.VMEM((m, nw), BF16),
            pltpu.VMEM((NT * V, n), BF16),
            pltpu.VMEM((NT * V, n), BF16),
            pltpu.VMEM((NT, V, L * cb), F32),
            pltpu.VMEM((NT, V, L * cb), F32),
            pltpu.VMEM((NT, Q, vb, L * cb), F32),
            pltpu.VMEM((NT, Q, vb, L * cb), F32),
            pltpu.VMEM((NT, L, vb, cb), F32),
            pltpu.VMEM((NT, L, vb, cb), F32),
            dma((R, Q)), dma((R, Q)), dma((L,)), dma((L, Q)), dma((L, 2)), dma((L, Q)),
            dma((Q, 2)), dma((Q, 2)),
            dma((K, R)), dma((K, 5)), dma((K, L)), dma((K, L)),
            dma((2,)),
            dma((NT, 2)), dma((NT, 2)), dma((NT, Q)), dma((NT, Q)), dma((NT, L)), dma((NT, L)),
        ],
        compiler_params=pltpu.CompilerParams(
            collective_id=0, has_side_effects=True, vmem_limit_bytes=67043328
        ),
    )(trials, valence_orb, conduction_orb, screened)


def solution(mesh):
    R, Q = mesh.shape["row"], mesh.shape["col"]
    placed = (P(None, "col", "row"), P("col", "row"), P("row", "col"), P("row", "col"))
    return jax.shard_map(
        functools.partial(body, R, Q), mesh=mesh, in_specs=placed,
        out_specs=P(None, "col", "row"), check_vma=False,
    )
```

```python
import functools

import jax
import jax.numpy as jnp
from jax import lax
from jax.experimental import pallas as pl
from jax.experimental.pallas import tpu as pltpu
from jax.sharding import PartitionSpec as P

F32 = jnp.float32
BF16 = jnp.bfloat16


def split(x):
    hi = x.astype(BF16)
    return hi, (x - hi.astype(F32)).astype(BF16)


def dot3(a_hi, a_lo, b_hi, b_lo, dims=((1,), (0,))):
    def one(a, b):
        return lax.dot_general(a, b, (dims, ((), ())), preferred_element_type=F32)

    return one(a_hi, b_hi) + (one(a_lo, b_hi) + one(a_hi, b_lo))


def kernel(
    R, Q, K,
    t_ref, v_ref, co_ref, s_hbm, out_ref,
    t_buf, t_hi, t_lo, v_all, v_hi, v_lo, vt_hi, vt_lo, co_buf, co_hi, co_lo, s_buf,
    p_hi, p_lo, u_hi, u_lo, psend, precv, osum, xrecv, zbuf, zrecv,
    t_recv, t_recv2, t_zs, t_xs, t_rs, t_ps, v_recv, v_send, co_recv, co_own, co_rel, co_fwd,
    s_sem, p_send, p_recv, x_send, x_recv, z_send, z_recv,
):
    NT, vb, cb = t_ref.shape
    V = vb * Q
    L = R // 2
    nw = co_buf.shape[3]
    row, q = lax.axis_index("row"), lax.axis_index("col")
    p, c = row // 2, row % 2
    mypos = c * L + p
    partner = (p * 2 + (1 - c), q)

    def line(pp):
        return (pp * 2 + c, q)

    def peer(qq):
        return (row, qq)

    def remote(src, dst, ss, rs, dev):
        return pltpu.make_async_remote_copy(
            src_ref=src, dst_ref=dst, send_sem=ss, recv_sem=rs,
            device_id=dev, device_id_type=pl.DeviceIdType.MESH,
        )

    barrier = pltpu.get_barrier_semaphore()
    others = [partner]
    others += [line((p + d) % L) for d in range(1, L)]
    others += [peer((q + d) % Q) for d in range(1, Q)]
    for dev in others:
        pl.semaphore_signal(barrier, inc=1, device_id=dev, device_id_type=pl.DeviceIdType.MESH)
    pl.semaphore_wait(barrier, len(others))

    def t_line(d):
        return remote(t_ref, t_buf.at[mypos, q], t_zs.at[d], t_recv.at[mypos, q], line((p + d) % L))

    square = Q == 4 and vb % 16 == 0
    sides = (q + 1 - 2 * (q % 2), (q + 2) % 4) if square else ()
    corner = 3 - q
    half_rows = [pl.ds(i * (vb // 2), vb // 2) for i in range(2)]

    def t_pos(j):
        return c * L + (p + L - j) % L

    def t_peer(j, d):
        pos = t_pos(j)
        src = t_ref if j == 0 else t_buf.at[pos, q]
        to = sides[d - 1] if square else (q + d) % Q
        return remote(src, t_buf.at[pos, q], t_xs.at[j, d], t_recv.at[pos, q], peer(to))

    def t_relay(j, i):
        part = t_buf.at[t_pos(j), sides[i], :, half_rows[i]]
        sem = t_recv if i == 0 else t_recv2
        return remote(part, part, t_rs.at[j, i], sem.at[t_pos(j), sides[i]], peer(sides[1 - i]))

    def t_corner_wait(j):
        for i in range(2):
            part = t_buf.at[t_pos(j), corner, :, half_rows[i]]
            sem = t_recv if i == 0 else t_recv2
            remote(part, part, t_zs.at[0], sem.at[t_pos(j), corner], partner).wait_recv()

    peers = range(1, 3 if square else Q)

    def t_partner(j, d):
        pos = c * L + (p + L - j) % L
        qq = (q, *sides, corner)[d] if square else (q + Q - d) % Q
        src = t_ref if (j == 0 and d == 0) else t_buf.at[pos, qq]
        return remote(src, t_buf.at[pos, qq], t_ps.at[j, d], t_recv.at[pos, qq], partner)

    def t_wait(pos, qq):
        remote(t_buf.at[pos, qq], t_buf.at[pos, qq], t_zs.at[0], t_recv.at[pos, qq], partner).wait_recv()

    def v_peer(d):
        return remote(v_ref, v_all.at[q], v_send.at[d, 0], v_recv.at[q, 0], peer((q + d) % Q))

    def v_side(i, part):
        rows = half_rows[part]
        return remote(
            v_ref.at[rows], v_all.at[q, rows], v_send.at[i, part], v_recv.at[q, part], peer(sides[i])
        )

    def v_relay(i):
        part = v_all.at[sides[i], half_rows[i]]
        return remote(part, part, v_send.at[2, i], v_recv.at[sides[i], i], peer(sides[1 - i]))

    def v_wait(qq, part):
        rows = v_all.at[qq, half_rows[part]]
        remote(rows, rows, v_send.at[0, 0], v_recv.at[qq, part], partner).wait_recv()

    def own_to(k, d):
        lanes = pl.ds(pl.multiple_of(k * nw, nw), nw)
        sign = 1 if d > 0 else -1
        return remote(
            co_ref.at[:, lanes], co_buf.at[k, mypos],
            co_own.at[k, abs(d) - 1 + (2 if sign < 0 else 0)], co_recv.at[k, mypos],
            line(jnp.clip(p + d, 0, L - 1)),
        )

    def own_partner(k):
        lanes = pl.ds(pl.multiple_of(k * nw, nw), nw)
        return remote(
            co_ref.at[:, lanes], co_buf.at[k, mypos], co_own.at[k, 4], co_recv.at[k, mypos], partner
        )

    def own_cases():
        for d in (1, 2):
            if d < L:
                yield d, p + d <= L - 1
                yield -d, p - d >= 0

    def send_own(k):
        for d, ok in own_cases():
            @pl.when(ok)
            def _():
                own_to(k, d).start()
        own_partner(k).start()

    def relay_right(pp):
        return jnp.logical_and(p - pp >= 2, p < L - 1)

    def relay_left(pp):
        return jnp.logical_and(pp - p >= 2, p > 0)

    def relay_copy(k, pp, to):
        pos = c * L + pp
        return remote(
            co_buf.at[k, pos], co_buf.at[k, pos], co_rel.at[k, pp], co_recv.at[k, pos],
            line(jnp.clip(to, 0, L - 1)),
        )

    def co_wait(k, pos):
        remote(co_buf.at[k, pos], co_buf.at[k, pos], co_own.at[k, 4], co_recv.at[k, pos], partner).wait_recv()

    def relay(k):
        for pp in range(L):
            for ok, to in ((relay_right(pp), p + 1), (relay_left(pp), p - 1)):
                @pl.when(ok)
                def _():
                    co_wait(k, c * L + pp)
                    relay_copy(k, pp, to).start()

    def fwd_copy(k, pp):
        pos = c * L + pp
        return remote(co_buf.at[k, pos], co_buf.at[k, pos], co_fwd.at[k, pp], co_recv.at[k, pos], partner)

    def forward(k):
        for pp in range(L):
            @pl.when(pp != p)
            def _():
                @pl.when(jnp.logical_not(jnp.logical_or(relay_right(pp), relay_left(pp))))
                def _():
                    co_wait(k, c * L + pp)
                fwd_copy(k, pp).start()

    def s_copy(k, slot):
        lanes = pl.ds(pl.multiple_of(k * nw, nw), nw)
        return pltpu.make_async_copy(s_hbm.at[:, lanes], s_buf.at[slot], s_sem.at[slot])

    for d in range(1, L):
        t_line(d).start()
    for d in peers:
        t_peer(0, d).start()
    t_partner(0, 0).start()
    if square:
        for i in range(2):
            v_side(i, i).start()
    ahead = [0]

    def more_own(k):
        while ahead[0] < min(k, K):
            send_own(ahead[0])
            ahead[0] += 1

    def more(fn, k):
        if k < K:
            fn(k)

    more_own(3)
    s_copy(0, 0).start()
    t_buf[mypos, q] = t_ref[...]
    v_all[q] = v_ref[...]
    for k in range(K):
        co_buf[k, mypos] = co_ref[:, k * nw : (k + 1) * nw]
    for j in range(1, L):
        t_wait(t_pos(j), q)
        for d in peers:
            t_peer(j, d).start()
        t_partner(j, 0).start()
    if square:
        for i in range(2):
            v_side(i, 1 - i).start()
        more(relay, 0)
        more_own(4)
        for j in range(L):
            for i in range(2):
                t_wait(t_pos(j), sides[i])
                t_relay(j, i).start()
                t_partner(j, 1 + i).start()
        for i in range(2):
            v_wait(sides[i], i)
            v_relay(i).start()
        for j in range(L):
            t_corner_wait(j)
            t_partner(j, 3).start()
    else:
        for d in range(1, Q):
            v_peer(d).start()
        more(relay, 0)
        more_own(4)
        for j in range(L):
            for d in range(1, Q):
                t_wait(t_pos(j), (q + Q - d) % Q)
                t_partner(j, d).start()
    more(relay, 1)
    more(forward, 0)
    more_own(5)
    for pp in range(L):
        for qq in range(Q):
            t_wait((1 - c) * L + pp, qq)
    for pos in range(R):
        for qq in range(Q):
            for t in range(NT):
                hi, lo = split(t_buf[pos, qq, t])
                rows, lanes = slice(t * V + qq * vb, t * V + (qq + 1) * vb), slice(pos * cb, (pos + 1) * cb)
                t_hi[rows, lanes] = hi
                t_lo[rows, lanes] = lo

    def lanes_of(k):
        return pl.ds(pl.multiple_of(k * nw, nw), nw)

    def encode_half(k):
        for pp in range(L):
            co_wait(k, (1 - c) * L + pp)
        lanes = lanes_of(k)
        for pos in range(R):
            hi, lo = split(co_buf[k, pos])
            co_hi[pos * cb : (pos + 1) * cb, lanes] = hi
            co_lo[pos * cb : (pos + 1) * cb, lanes] = lo
        half = dot3(t_hi[...], t_lo[...], co_hi[:, lanes], co_lo[:, lanes])
        hi, lo = split(half)
        u_hi[:, lanes] = hi
        u_lo[:, lanes] = lo

    def project(slot, k, t):
        lanes = lanes_of(k)
        rows = pl.ds(pl.multiple_of(t * V, V), V)
        h_hi, h_lo = u_hi[rows, lanes], u_lo[rows, lanes]
        m = s_buf.shape[1]
        step = min(256, m)
        for r in range(0, m, step):
            block = slice(r, r + step)
            hi, lo = split(s_buf[slot, block] * dot3(vt_hi[block], vt_lo[block], h_hi, h_lo))
            p_hi[block] = hi
            p_lo[block] = lo
        step = min(256, V)
        for r in range(0, V, step):
            hi, lo = split(dot3(v_hi[r : r + step], v_lo[r : r + step], p_hi[...], p_lo[...]))
            rows = pl.ds(pl.multiple_of(t * V + r, step), step)
            u_hi[rows, lanes] = hi
            u_lo[rows, lanes] = lo

    more_own(6)
    encode_half(0)
    more(relay, 2)
    more(forward, 1)
    more_own(7)
    more(encode_half, 1)
    if square:
        for i in range(2):
            v_wait(sides[i], 1 - i)
        for i in range(2):
            v_wait(corner, i)
    else:
        for d in range(1, Q):
            qq = (q + Q - d) % Q
            remote(v_all.at[qq], v_all.at[qq], v_send.at[0, 0], v_recv.at[qq, 0], partner).wait_recv()
    for qq in range(Q):
        hi, lo = split(v_all[qq])
        v_hi[qq * vb : (qq + 1) * vb, :] = hi
        v_lo[qq * vb : (qq + 1) * vb, :] = lo
    hi, lo = split(v_all[...].reshape(V, v_all.shape[2]).T)
    vt_hi[...] = hi
    vt_lo[...] = lo

    both = K // 2
    steps = both + NT * (K - both)

    def next_screened(i):
        @pl.when(i + 1 < steps)
        def _():
            later = jnp.where(i + 1 < both, i + 1, both + (i + 1 - both) % (K - both))
            s_copy(later, (i + 1) % 2).start()

    def stage(s, carry):
        @pl.when(s + 7 < K)
        def _():
            send_own(s + 7)

        @pl.when(s + 3 < K)
        def _():
            relay(s + 3)

        @pl.when(s + 2 < K)
        def _():
            forward(s + 2)

        s_copy(s, s % 2).wait()
        next_screened(s)

        def one(t, carry):
            project(s % 2, s, t)
            return carry

        carry = lax.fori_loop(0, jnp.where(s < both, NT, 1), one, carry)

        @pl.when(s + 2 < K)
        def _():
            encode_half(s + 2)

        return carry

    lax.fori_loop(0, K, stage, 0)

    half_c = L * cb

    parts = 2 if Q % 2 == 0 else 1
    pq = Q // parts
    pv = V // parts

    def side_of(h):
        return (q // pq + parts - 1 - h) % parts

    def part_rows(h):
        return pl.ds(pl.multiple_of(side_of(h) * pv, pv), pv)

    def decode(t, par, h):
        rows = pl.ds(pl.multiple_of(t * V + side_of(h) * pv, pv), pv)
        cols = pl.ds(pl.multiple_of(par * half_c, half_c), half_c)
        return dot3(u_hi[rows, :], u_lo[rows, :], co_hi[cols, :], co_lo[cols, :], ((1,), (1,)))

    def p_copy(t, h):
        rows = part_rows(h)
        return remote(psend.at[t, rows], precv.at[t, rows], p_send.at[t, h], p_recv.at[t, h], partner)

    def peer_at(h, i):
        return side_of(h) * pq + (q + i) % pq

    def x_copy(t, h, i):
        to = peer_at(h, i)
        e = h * pq + i
        return remote(osum.at[t, to], xrecv.at[t, e], x_send.at[t, e], x_recv.at[t, e], peer(to))

    hops = [(h, i) for h in range(parts) for i in range(pq) if h < parts - 1 or i > 0]

    def x_wait(t, h, i):
        e = h * pq + i
        remote(xrecv.at[t, e], xrecv.at[t, e], x_send.at[t, e], x_recv.at[t, e], partner).wait_recv()

    def z_copy(t, d):
        to = (p + d) % L
        return remote(zbuf.at[t, to], zrecv.at[t, d], z_send.at[t, d], z_recv.at[t, d], line(to))

    def to_partner(t, h):
        psend[t, part_rows(h)] = decode(t, 1 - c, h)
        p_copy(t, h).start()

    def to_peers(t, h):
        own = decode(t, c, h)
        p_copy(t, h).wait_recv()
        for i in range(pq):
            qq = side_of(h) * pq + i
            rows = pl.ds(pl.multiple_of(qq * vb, vb), vb)
            osum[t, qq] = own[i * vb : (i + 1) * vb, :] + precv[t, rows, :]
        for g, i in hops:
            if g == h:
                x_copy(t, g, i).start()

    def to_line(t):
        total = osum[t, q]
        for h, i in hops:
            x_wait(t, h, i)
            total = total + xrecv[t, h * pq + i]
        for pp in range(L):
            zbuf[t, pp] = total[:, pp * cb : (pp + 1) * cb]
        for d in range(1, L):
            z_copy(t, d).start()

    def finish(t):
        final = zbuf[t, p]
        for d in range(1, L):
            z_copy(t, d).wait_recv()
            final = final + zrecv[t, d]
        out_ref[t] = final

    for t in range(NT):
        if t > 0:
            def later_stage(s, carry):
                i = both + t * (K - both) + s
                s_copy(both + s, i % 2).wait()
                next_screened(i)
                project(i % 2, both + s, t)
                return carry

            lax.fori_loop(0, K - both, later_stage, 0)
        to_partner(t, 0)
        if t > 0:
            to_line(t - 1)
        for h in range(parts):
            to_peers(t, h)
            if h + 1 < parts:
                to_partner(t, h + 1)
    to_line(NT - 1)
    for t in range(NT):
        finish(t)

    for d in range(1, L):
        t_line(d).wait_send()
        for t in range(NT):
            z_copy(t, d).wait_send()
    for t in range(NT):
        for h, i in hops:
            x_copy(t, h, i).wait_send()
    if square:
        for i in range(2):
            v_relay(i).wait_send()
            for part in range(2):
                v_side(i, part).wait_send()
    else:
        for d in range(1, Q):
            v_peer(d).wait_send()
    for t in range(NT):
        for h in range(parts):
            p_copy(t, h).wait_send()
    for j in range(L):
        for d in peers:
            t_peer(j, d).wait_send()
        if square:
            for i in range(2):
                t_relay(j, i).wait_send()
        for d in range(Q):
            t_partner(j, d).wait_send()

    def drain(k, carry):
        for d, ok in own_cases():
            @pl.when(ok)
            def _():
                own_to(k, d).wait_send()
        own_partner(k).wait_send()
        for pp in range(L):
            for ok, to in ((relay_right(pp), p + 1), (relay_left(pp), p - 1)):
                @pl.when(ok)
                def _():
                    relay_copy(k, pp, to).wait_send()

            @pl.when(pp != p)
            def _():
                fwd_copy(k, pp).wait_send()
        return carry

    lax.fori_loop(0, K, drain, 0)


def body(R, Q, trials, valence_orb, conduction_orb, screened):
    NT, vb, cb = trials.shape
    m = valence_orb.shape[1]
    n = conduction_orb.shape[1]
    V, C, L = vb * Q, cb * R, R // 2
    nw = min(256, n)
    K = n // nw
    dma = pltpu.SemaphoreType.DMA
    vm = pl.BlockSpec(memory_space=pltpu.VMEM)
    return pl.pallas_call(
        functools.partial(kernel, R, Q, K),
        out_shape=jax.ShapeDtypeStruct((NT, vb, cb), F32),
        in_specs=[vm, vm, vm, pl.BlockSpec(memory_space=pl.ANY)],
        out_specs=vm,
        scratch_shapes=[
            pltpu.VMEM((R, Q, NT, vb, cb), F32),
            pltpu.VMEM((NT * V, C), BF16),
            pltpu.VMEM((NT * V, C), BF16),
            pltpu.VMEM((Q, vb, m), F32),
            pltpu.VMEM((V, m), BF16),
            pltpu.VMEM((V, m), BF16),
            pltpu.VMEM((m, V), BF16),
            pltpu.VMEM((m, V), BF16),
            pltpu.VMEM((K, R, cb, nw), F32),
            pltpu.VMEM((C, n), BF16),
            pltpu.VMEM((C, n), BF16),
            pltpu.VMEM((2, m, nw), F32),
            pltpu.VMEM((m, nw), BF16),
            pltpu.VMEM((m, nw), BF16),
            pltpu.VMEM((NT * V, n), BF16),
            pltpu.VMEM((NT * V, n), BF16),
            pltpu.VMEM((NT, V, L * cb), F32),
            pltpu.VMEM((NT, V, L * cb), F32),
            pltpu.VMEM((NT, Q, vb, L * cb), F32),
            pltpu.VMEM((NT, Q, vb, L * cb), F32),
            pltpu.VMEM((NT, L, vb, cb), F32),
            pltpu.VMEM((NT, L, vb, cb), F32),
            dma((R, Q)), dma((R, Q)), dma((L,)), dma((L, Q)), dma((L, 2)), dma((L, Q)),
            dma((Q, 2)), dma((Q, 2)),
            dma((K, R)), dma((K, 5)), dma((K, L)), dma((K, L)),
            dma((2,)),
            dma((NT, 2)), dma((NT, 2)), dma((NT, Q)), dma((NT, Q)), dma((NT, L)), dma((NT, L)),
        ],
        compiler_params=pltpu.CompilerParams(
            collective_id=0, has_side_effects=True, vmem_limit_bytes=67043328
        ),
    )(trials, valence_orb, conduction_orb, screened)


def solution(mesh):
    R, Q = mesh.shape["row"], mesh.shape["col"]
    placed = (P(None, "col", "row"), P("col", "row"), P("row", "col"), P("row", "col"))
    return jax.shard_map(
        functools.partial(body, R, Q), mesh=mesh, in_specs=placed,
        out_specs=P(None, "col", "row"), check_vma=False,
    )
```
